32 devices in a mesh: lat: 4 (over y, x), lon: 8 (over z, core).
Axes of the slice: x: 2, y: 2, z: 4, core: 2. Of those that a mesh axis runs over, the one named last changes fastest.
Arguments:
- fine_nodes: float32 [2, 128, 256, 512], P(None, 'lat', 'lon'), may hold values from -6 to 6
- mid_nodes: float32 [2, 32, 64, 512], P(None, 'lat', 'lon'), may hold values from -6 to 6
- coarse_nodes: float32 [2, 8, 16, 512], P(None, 'lat', 'lon'), may hold values from -6 to 6
- edge_flags: int32 [8, 128, 256], P(None, 'lat', 'lon'), may hold values 0 or 1
- proc_weights: bfloat16 [3, 4, 512, 512], replicated, may hold values from -0.25 to 0.25
- bridge_weights: bfloat16 [4, 512, 512], replicated, may hold values from -0.25 to 0.25
- proc_biases: float32 [3, 512], replicated, may hold values from -3 to 3
Outputs:
- refined: float32 [2, 128, 256, 512], P(None, 'lat', 'lon')
- fine_average: bfloat16 [2, 128, 256, 512], P(None, 'lat', 'lon')
The draws below stay inside these ranges and needn't reach their ends.
All inputs are finite; a program needn't handle non-finite values. No bound on the sum of `edge_flags` on one device may be relied on, other than what follows from the above.
Results may differ from the reference program's by a relative error of at most 0.005.
Values may be sent and summed in bfloat16 or wider, within the bound.
A program may use at most 128 MiB of HBM per device.

```python
import jax
import jax.numpy as jnp
from jax import lax

D = 512
SAMPLES = 2
NF_LAT = 128
NF_LON = 256
NM_LAT = 32
NM_LON = 64
NC_LAT = 8
NC_LON = 16


def with_ends(values, rng, least, high):
    place = [jax.random.randint(jax.random.fold_in(rng, axis), (), 0, length) for axis, length in enumerate(values.shape)]
    longest = values.shape.index(max(values.shape))
    beside = place[:longest] + [(place[longest] + 1) % values.shape[longest]] + place[longest + 1:]
    return values.at[tuple(place)].set(least).at[tuple(beside)].set(high)


def block_scale(rng, shape, shards, smallest, top_value):
    level = 1.0
    for position, blocks in shards:
        draws = jax.random.uniform(jax.random.fold_in(jax.random.fold_in(rng, 6), position), (blocks,), jnp.float32, smallest / len(shards), top_value / len(shards))
        level = level * jnp.repeat(jnp.exp(draws), shape[position] // blocks).reshape((-1,) + (1,) * (len(shape) - 1 - position))
    return level


def scatter_about(key, dims, scale, reach, split=(), dtype=jnp.bfloat16):
    level = block_scale(key, dims, split, -0.22, 0.18) if split else 1.0
    values = jax.random.normal(key, dims, jnp.float32) * scale * level
    return jnp.minimum(jnp.maximum(values, -reach), reach).astype(dtype)


def setup_inputs(seed: int = 0) -> dict:
    keys = jax.random.split(jax.random.key(seed), 8)
    return {
        "fine_nodes": scatter_about(keys[0], (SAMPLES, NF_LAT, NF_LON, D), 1.0, 6.0, ((1, 4), (2, 8)), jnp.float32),
        "mid_nodes": scatter_about(keys[1], (SAMPLES, NM_LAT, NM_LON, D), 1.0, 6.0, ((1, 4), (2, 8)), jnp.float32),
        "coarse_nodes": scatter_about(keys[2], (SAMPLES, NC_LAT, NC_LON, D), 1.0, 6.0, ((1, 4), (2, 8)), jnp.float32),
        "edge_flags": with_ends((jax.random.randint(keys[3], (8, NF_LAT, NF_LON), 0, 8) < 7).astype(jnp.int32), jax.random.fold_in(keys[3], 1), 0, 1),
        "proc_weights": scatter_about(keys[4], (3, 4, D, D), D ** -0.5, 0.25),
        "bridge_weights": scatter_about(keys[5], (4, D, D), D ** -0.5, 0.25),
        "proc_biases": scatter_about(keys[6], (3, D), 0.5, 3.0, (), jnp.float32),
    }


offsets = ((-1, -1), (-1, 0), (-1, 1), (0, -1), (0, 1), (1, -1), (1, 0), (1, 1))


def neighbour(values, step_lat, step_lon):
    rows = values.shape[0]
    padded = jnp.pad(values, ((1, 1), (0, 0), (0, 0)))
    shifted = padded[1 + step_lat:1 + step_lat + rows]
    return jnp.roll(shifted, -step_lon, axis=1)


def project(values, matrix):
    shape = values.shape
    flat = values.reshape(-1, shape[-1])
    result = jnp.dot(flat, matrix, preferred_element_type=jnp.float32)
    return result.reshape(shape[:-1] + (matrix.shape[1],))


def level_pass(states, flag_grid, weights, biases):
    rows = states.shape[0]
    operand = states.astype(jnp.bfloat16)
    receiver = project(operand, weights[0])
    sender = project(operand, weights[1]).astype(jnp.bfloat16)
    row_ids = jnp.arange(rows)
    summed = jnp.zeros(states.shape, jnp.float32)
    for direction, (step_lat, step_lon) in enumerate(offsets):
        inside = ((row_ids + step_lat >= 0) & (row_ids + step_lat < rows)).astype(jnp.float32)[:, None]
        if flag_grid is None:
            usable = inside
        else:
            usable = inside * flag_grid[direction].astype(jnp.float32)
        nearby = neighbour(sender, step_lat, step_lon).astype(jnp.float32)
        hidden = jax.nn.silu(receiver + nearby + biases).astype(jnp.bfloat16)
        message = jax.nn.silu(project(hidden, weights[2]))
        summed = summed + usable[:, :, None] * message
    average = (summed * 0.125).astype(jnp.bfloat16)
    return states + project(average, weights[3]), average


def pooled(states):
    rows, cols, features = states.shape
    blocks = states.reshape(rows // 4, 4, cols // 4, 4, features)
    return jnp.mean(blocks, axis=(1, 3)).astype(jnp.bfloat16)


def expand(values):
    return jnp.repeat(jnp.repeat(values, 4, axis=0), 4, axis=1)


def reference(fine_nodes, mid_nodes, coarse_nodes, edge_flags, proc_weights, bridge_weights, proc_biases):
    def single(packed):
        fine_state, mid_state, coarse_state = packed
        fine_one, fine_average = level_pass(fine_state, edge_flags, proc_weights[0], proc_biases[0])
        mid_zero = mid_state + jax.nn.silu(project(pooled(fine_one), bridge_weights[0]))
        mid_one, unused_mid = level_pass(mid_zero, None, proc_weights[1], proc_biases[1])
        coarse_zero = coarse_state + jax.nn.silu(project(pooled(mid_one), bridge_weights[1]))
        coarse_one, unused_coarse = level_pass(coarse_zero, None, proc_weights[2], proc_biases[2])
        lifted = jax.nn.silu(project(coarse_one.astype(jnp.bfloat16), bridge_weights[2]))
        mid_two = mid_one + expand(lifted)
        spread = jax.nn.silu(project(mid_two.astype(jnp.bfloat16), bridge_weights[3]))
        return fine_one + expand(spread), fine_average

    return lax.map(single, (fine_nodes, mid_nodes, coarse_nodes))
```

```python
import functools

import jax
import jax.numpy as jnp
import numpy as np
from jax import lax
from jax.experimental import pallas as pl
from jax.experimental.pallas import tpu as pltpu
from jax.sharding import PartitionSpec as P

offsets = ((-1, -1), (-1, 0), (-1, 1), (0, -1), (0, 1), (1, -1), (1, 0), (1, 1))
bf16 = jnp.bfloat16
f32 = jnp.float32


def mm(a, b):
    return jnp.dot(a, b, preferred_element_type=f32)


def half_silu(u):
    return u * jnp.tanh(u) + u


def silu(x):
    return half_silu(x * 0.5)


def fine_kernel(
    dims,
    x_hbm, w_ref, b_ref, flag_ref, pool_ref, lat_ref, lon_ref, cor_ref,
    one_ref, avg_ref, pool_out,
    recv, shifted, w2h, x_buf, sems,
):
    samples, rows, cols, d, step = dims
    per = rows // step
    chunk = step * cols
    chunks = samples * per
    copies = [
        pltpu.make_async_copy(x_hbm.at[pl.ds(c * chunk, chunk)], x_buf.at[pl.ds(c * chunk, chunk)], sems.at[c])
        for c in range(chunks)
    ]
    for copy in copies:
        copy.start()
    w2h[...] = w_ref[2] * jnp.asarray(0.5, bf16)
    bias = b_ref[...] * 0.5
    half = jnp.asarray(0.5, bf16)
    w1 = w_ref[1]

    def place(s, low, high, b, top, count):
        size = count * cols
        col = lax.broadcasted_iota(jnp.int32, (size, d), 0) % cols
        left = jnp.broadcast_to(low[:, None, :], (count, cols, d)).reshape(size, d)
        right = jnp.broadcast_to(high[:, None, :], (count, cols, d)).reshape(size, d)
        minus = jnp.where(col == 0, left, pltpu.roll(s, 1, 0))
        plus = jnp.where(col == cols - 1, right, pltpu.roll(s, size - 1, 0))
        window = pl.ds(top * cols, size)
        shifted[0, b, window, :] = minus.astype(bf16)
        shifted[1, b, window, :] = s.astype(bf16)
        shifted[2, b, window, :] = plus.astype(bf16)

    lat_s = mm(lat_ref[...] * half, w1)
    lon_s = mm(lon_ref[...] * half, w1)
    cor_s = mm(cor_ref[...] * half, w1)
    for b in range(samples):
        for side in range(2):
            at = (side * samples + b) * cols
            corner = (side * samples + b) * 2
            place(
                lat_s[at : at + cols], cor_s[corner : corner + 1], cor_s[corner + 1 : corner + 2],
                b, side * (rows + 1), 1,
            )
    for c in range(chunks):
        b, part = divmod(c, per)
        copies[c].wait()
        window = pl.ds(c * chunk, chunk)
        xh = x_buf[window, :].astype(bf16) * half
        recv[window, :] = (mm(xh, w_ref[0]) + bias).astype(bf16)
        s = mm(xh, w1)
        at = b * rows + part * step
        place(
            s, lon_s[at : at + step], lon_s[samples * rows + at : samples * rows + at + step],
            b, 1 + part * step, step,
        )

    def body(c, carry):
        b = c // per
        part = c % per
        window = pl.ds(pl.multiple_of(c * chunk, chunk), chunk)
        flags = flag_ref[pl.ds(pl.multiple_of(part * chunk, chunk), chunk), :]
        r = recv[window, :]
        total = jnp.zeros((chunk, d), f32)
        for k, (p, q) in enumerate(offsets):
            start = pl.multiple_of((part * step + 1 + p) * cols, cols)
            u = r + shifted[q + 1, b, pl.ds(start, chunk), :]
            z = mm(half_silu(u), w2h[...]).astype(bf16)
            live = jnp.broadcast_to(flags[:, k : k + 1], (chunk, 128)).astype(bf16)
            live = jnp.concatenate([live] * (d // 128), axis=1)
            total = total + (half_silu(z) * live).astype(f32)
        average = (total * 0.125).astype(bf16)
        avg_ref[window, :] = average
        one = x_buf[window, :] + mm(average, w_ref[3])
        one_ref[window, :] = one
        small = chunk // 16
        pool_out[pl.ds(pl.multiple_of(c * small, small), small), :] = mm(pool_ref[...], one.astype(bf16))
        return carry

    lax.fori_loop(0, chunks, body, 0)


def swap(value, step_lat, step_lon):
    lats, lons = lax.axis_size("lat"), lax.axis_size("lon")
    pairs = [
        (((i + step_lat) % lats) * lons + (j + step_lon) % lons, i * lons + j)
        for i in range(lats)
        for j in range(lons)
    ]
    return lax.ppermute(value, ("lat", "lon"), pairs)


def fine_pass(nodes, edge_flags, weights, biases):
    samples, rows, cols, d = nodes.shape
    step = 8
    chunk = step * cols
    lat, lats = lax.axis_index("lat"), lax.axis_size("lat")
    edge = nodes[:, rows - 1].astype(bf16)
    north = swap(edge, -1, 0)
    nw, ne = swap(edge[:, cols - 1], -1, -1), swap(edge[:, 0], -1, 1)
    edge = nodes[:, 0].astype(bf16)
    south = swap(edge, 1, 0)
    sw, se = swap(edge[:, cols - 1], 1, -1), swap(edge[:, 0], 1, 1)
    west = swap(nodes[:, :, cols - 1].astype(bf16), 0, -1)
    east = swap(nodes[:, :, 0].astype(bf16), 0, 1)
    lat_halo = jnp.concatenate([north, south]).reshape(-1, d)
    lon_halo = jnp.concatenate([west, east]).reshape(-1, d)
    corners = jnp.stack([jnp.stack([nw, ne], 1), jnp.stack([sw, se], 1)]).reshape(-1, d)
    corners = jnp.pad(corners, ((0, -corners.shape[0] % 16), (0, 0)))
    row = lat * rows + jnp.arange(rows, dtype=jnp.int32)
    p = jnp.array([o[0] for o in offsets], jnp.int32)[:, None]
    inside = (row + p >= 0) & (row + p < rows * lats)
    live = jnp.where(inside[:, :, None], edge_flags, 0).astype(f32)
    live = live.reshape(8, rows * cols).T
    n = np.arange(chunk)
    parent = (n // cols // 4) * (cols // 4) + (n % cols) // 4
    pool = jnp.asarray((parent[None, :] == np.arange(chunk // 16)[:, None]) / 16.0, bf16)
    total = samples * rows * cols
    vmem = pl.BlockSpec(memory_space=pltpu.VMEM)
    return pl.pallas_call(
        functools.partial(fine_kernel, (samples, rows, cols, d, step)),
        out_shape=(
            jax.ShapeDtypeStruct((total, d), f32),
            jax.ShapeDtypeStruct((total, d), bf16),
            jax.ShapeDtypeStruct((total // 16, d), f32),
        ),
        in_specs=[pl.BlockSpec(memory_space=pl.ANY)] + [vmem] * 7,
        out_specs=(vmem, vmem, vmem),
        scratch_shapes=[
            pltpu.VMEM((total, d), bf16),
            pltpu.VMEM((3, samples, (rows + 2) * cols, d), bf16),
            pltpu.VMEM((d, d), bf16),
            pltpu.VMEM((total, d), f32),
            pltpu.SemaphoreType.DMA((total // chunk,)),
        ],
        compiler_params=pltpu.CompilerParams(vmem_limit_bytes=60 << 20),
        name="fine",
    )(nodes.reshape(total, d), weights, biases[None], live, pool, lat_halo, lon_halo, corners)


def padded_2(block, sides, width):
    for axis, dim in sides:
        count = lax.axis_size(axis)
        forward = [(i, i + 1) for i in range(count - 1)]
        forward.append((count - 1, 0))
        backward = [(target, source) for source, target in forward]
        low = lax.ppermute(
            lax.slice_in_dim(block, block.shape[dim] - width, None, axis=dim), axis, forward
        )
        high = lax.ppermute(lax.slice_in_dim(block, 0, width, axis=dim), axis, backward)
        block = jnp.concatenate([low, block, high], axis=dim)
    return block


def project(values, matrix):
    shape = values.shape
    result = mm(values.reshape(-1, shape[-1]), matrix)
    return result.reshape(shape[:-1] + (matrix.shape[1],))


def level_pass(states, weights, biases, row_start, total_rows):
    rows = states.shape[1]
    cols = states.shape[2]
    operand = states.astype(bf16)
    receiver = project(operand, weights[0])
    sender = project(operand, weights[1]).astype(bf16)
    padded = padded_2(sender, (("lat", 1), ("lon", 2)), 1)
    row_ids = row_start + jnp.arange(rows, dtype=jnp.int32)
    summed = jnp.zeros(states.shape, f32)
    for p, q in offsets:
        usable = ((row_ids + p >= 0) & (row_ids + p < total_rows)).astype(f32)[:, None]
        nearby = padded[:, 1 + p : 1 + p + rows, 1 + q : 1 + q + cols].astype(f32)
        hidden = jax.nn.silu(receiver + nearby + biases).astype(bf16)
        message = jax.nn.silu(project(hidden, weights[2]))
        summed = summed + usable[None, :, :, None] * message
    average = (summed * 0.125).astype(bf16)
    return states + project(average, weights[3])


def pooled(states):
    samples, rows, cols, features = states.shape
    blocks = states.reshape(samples, rows // 4, 4, cols // 4, 4, features)
    return jnp.mean(blocks, axis=(2, 4)).astype(bf16)


def expand(values):
    return jnp.repeat(jnp.repeat(values, 4, axis=1), 4, axis=2)


def local(
    fine_nodes, mid_nodes, coarse_nodes, edge_flags, proc_weights, bridge_weights, proc_biases
):
    lat_index = lax.axis_index("lat")
    lat_count = lax.axis_size("lat")
    mid_rows = mid_nodes.shape[1]
    coarse_rows = coarse_nodes.shape[1]
    one, average, pool = fine_pass(fine_nodes, edge_flags, proc_weights[0], proc_biases[0])
    fine_one = one.reshape(fine_nodes.shape)
    pool = pool.reshape(mid_nodes.shape).astype(bf16)
    mid_zero = mid_nodes + jax.nn.silu(project(pool, bridge_weights[0]))
    mid_one = level_pass(
        mid_zero, proc_weights[1], proc_biases[1], lat_index * mid_rows, mid_rows * lat_count
    )
    coarse_zero = coarse_nodes + jax.nn.silu(project(pooled(mid_one), bridge_weights[1]))
    coarse_one = level_pass(
        coarse_zero, proc_weights[2], proc_biases[2], lat_index * coarse_rows, coarse_rows * lat_count
    )
    lifted = jax.nn.silu(project(coarse_one.astype(bf16), bridge_weights[2]))
    mid_two = mid_one + expand(lifted)
    spread = jax.nn.silu(project(mid_two.astype(bf16), bridge_weights[3]))
    return (fine_one + expand(spread), average.reshape(fine_nodes.shape))


def solution(mesh):
    placed = (
        P(None, "lat", "lon", None),
        P(None, "lat", "lon", None),
        P(None, "lat", "lon", None),
        P(None, "lat", "lon"),
        P(),
        P(),
        P(),
    )
    return jax.shard_map(
        local,
        mesh=mesh,
        in_specs=placed,
        out_specs=(P(None, "lat", "lon", None), P(None, "lat", "lon", None)),
        check_vma=False,
    )
```

```python
import functools

import jax
import jax.numpy as jnp
import numpy as np
from jax import lax
from jax.experimental import pallas as pl
from jax.experimental.pallas import tpu as pltpu
from jax.sharding import PartitionSpec as P

offsets = ((-1, -1), (-1, 0), (-1, 1), (0, -1), (0, 1), (1, -1), (1, 0), (1, 1))
bf16 = jnp.bfloat16
f32 = jnp.float32
MESH = pl.DeviceIdType.MESH
LANES = 128
EDGE = 16


def mm(a, b):
    return jnp.dot(a, b, preferred_element_type=f32)


def half_silu(u):
    return u * jnp.tanh(u) + u


def silu(x):
    return half_silu(x * 0.5)


def edge_of(step, count):
    if step == 0:
        return list(range(count))
    return [count - 1] if step < 0 else [0]


def small_tables(samples, rows, cols):
    nodes = samples * rows * cols
    padded = -(-nodes // 16) * 16
    pick = np.zeros((8 * EDGE, padded), np.float32)
    slot = {}
    for k, (p, q) in enumerate(offsets):
        e = 0
        for b in range(samples):
            for i in edge_of(p, rows):
                for j in edge_of(q, cols):
                    pick[k * EDGE + e, (b * rows + i) * cols + j] = 1
                    slot[k, b, i, j] = padded + k * EDGE + e
                    e += 1
        assert e <= EDGE
    gather = np.zeros((8, padded, padded + 8 * EDGE), np.float32)
    for k, (p, q) in enumerate(offsets):
        for b in range(samples):
            for i in range(rows):
                for j in range(cols):
                    a, c = i + p, j + q
                    over = (-1 if a < 0 else int(a >= rows), -1 if c < 0 else int(c >= cols))
                    if over == (0, 0):
                        source = (b * rows + a) * cols + c
                    else:
                        source = slot[offsets.index(over), b, a % rows, c % cols]
                    gather[k, (b * rows + i) * cols + j, source] = 1
    return jnp.asarray(pick, bf16), jnp.asarray(gather.reshape(8 * padded, -1), bf16)


def pool_table(rows, cols, out_rows):
    n = np.arange(rows * cols)
    parent = (n // cols // 4) * (cols // 4) + (n % cols) // 4
    return (parent[None, :] == np.arange(out_rows)[:, None]).astype(np.float32)


def sweep_kernel(
    dims,
    x_hbm, mid_ref, coarse_ref, flag_ref, proc_hbm, bridge_hbm, bias_ref,
    pool_ref, place_ref, row_ref, count_ref,
    pick_mid, gather_mid, pick_coarse, gather_coarse, pool_mid, spread_mid,
    one_hbm, avg_hbm, spread_ref,
    recv, shifted, x_buf, one_buf, avg_buf, w, w2h, live_buf, pool_buf,
    out_buf, halo, mid_send, mid_full, coarse_send, coarse_full, mid_hidden, coarse_hidden,
    x_sems, w_sems, one_sems, avg_sems, send_sems, recv_sems,
):
    samples, rows, cols, d, step, mid_dims, coarse_dims = dims
    per = rows // step
    chunk = step * cols
    chunks = samples * per
    lat, lon = lax.axis_index("lat"), lax.axis_index("lon")
    lats, lons = lax.axis_size("lat"), lax.axis_size("lon")
    half = jnp.asarray(0.5, bf16)

    def target(k):
        p, q = offsets[k]
        return (lax.rem(lat - p + lats, lats), lax.rem(lon - q + lons, lons))

    barrier = pltpu.get_barrier_semaphore()
    for k in range(8):
        pl.semaphore_signal(barrier, inc=1, device_id=target(k), device_id_type=MESH)
    copies = [
        pltpu.make_async_copy(x_hbm.at[pl.ds(c * chunk, chunk)], x_buf.at[pl.ds(c * chunk, chunk)], x_sems.at[c])
        for c in range(chunks)
    ]
    loads = [pltpu.make_async_copy(proc_hbm.at[0], w.at[pl.ds(0, 4)], w_sems.at[0])]
    loads += [pltpu.make_async_copy(proc_hbm.at[1], w.at[pl.ds(4, 4)], w_sems.at[1])]
    loads += [pltpu.make_async_copy(proc_hbm.at[2], w.at[pl.ds(8, 4)], w_sems.at[2])]
    loads += [pltpu.make_async_copy(bridge_hbm, w.at[pl.ds(12, 4)], w_sems.at[3])]
    for copy in copies + loads:
        copy.start()

    table = jnp.zeros((rows, 8 * cols), f32)
    for k in range(8):
        table = table + mm(flag_ref[k].astype(bf16), place_ref[k])
    spread_flags = mm(row_ref[...], table.astype(bf16))
    node = lax.broadcasted_iota(jnp.int32, spread_flags.shape, 0)
    lane = lax.broadcasted_iota(jnp.int32, spread_flags.shape, 1)
    own = jnp.where(node % cols == lane % cols, spread_flags, 0.0).astype(bf16)
    live = mm(own, count_ref[...])
    node = lax.broadcasted_iota(jnp.int32, live.shape, 0) // cols
    lane = lax.broadcasted_iota(jnp.int32, live.shape, 1)
    top = jnp.where(lat == 0, 0, -1)
    bottom = jnp.where(lat == lats - 1, rows - 1, -1)
    live_buf[...] = jnp.where(
        ((lane < 3) & (node == top)) | ((lane > 4) & (node == bottom)), 0.0, live
    )

    for copy in copies:
        copy.wait()
    base = {1: 0, 6: samples * cols, 3: 2 * samples * cols, 4: 2 * samples * cols + samples * rows}
    size = {1: samples * cols, 6: samples * cols, 3: samples * rows, 4: samples * rows}
    corner = 2 * samples * (cols + rows)
    for n, k in enumerate((0, 2, 5, 7)):
        base[k], size[k] = corner + n * EDGE, EDGE
    per_sample = rows * cols
    grid_buf = x_buf.reshape(samples * rows, cols, d)
    row16 = lax.broadcasted_iota(jnp.int32, (EDGE, d), 0)
    for k, (p, q) in enumerate(offsets):
        i, j = edge_of(p, rows)[0], edge_of(q, cols)[0]
        if p == 0:
            out_buf[pl.ds(base[k], size[k]), :] = grid_buf[:, j, :].astype(bf16)
        elif q == 0:
            for b in range(samples):
                out_buf[pl.ds(base[k] + b * cols, cols), :] = x_buf[
                    pl.ds(b * per_sample + i * cols, cols), :
                ].astype(bf16)
        else:
            value = jnp.zeros((EDGE, d), f32)
            for b in range(samples):
                at = b * per_sample + i * cols + j
                value = jnp.where(row16 == b, jnp.broadcast_to(x_buf[at : at + 1, :], (EDGE, d)), value)
            out_buf[pl.ds(base[k], EDGE), :] = value.astype(bf16)
    pl.semaphore_wait(barrier, 8)

    def exchange(level, source, dest, spans, shift):
        sends = []
        for k in range(8):
            at, count = spans[k]
            sends.append(
                pltpu.make_async_remote_copy(
                    src_ref=source.at[pl.ds(at, count)],
                    dst_ref=dest.at[pl.ds(shift + at, count)],
                    send_sem=send_sems.at[level * 8 + k],
                    recv_sem=recv_sems.at[level * 8 + k],
                    device_id=target(k),
                    device_id_type=MESH,
                )
            )
        for send in sends:
            send.start()
        return sends

    sends = exchange(0, out_buf, halo, {k: (base[k], size[k]) for k in range(8)}, 0)

    loads[0].wait()
    w2h[0] = w[2] * half
    bias = bias_ref[0:1, :] * 0.5

    def project_body(c, carry):
        window = pl.ds(pl.multiple_of(c * chunk, chunk), chunk)
        xh = x_buf[window, :].astype(bf16) * half
        recv[window, :] = (mm(xh, w[0]) + bias).astype(bf16)
        one_buf[window, :] = mm(xh, w[1])
        return carry

    lax.fori_loop(0, chunks, project_body, 0)
    for send in sends:
        send.wait()
    hs = mm(halo[...] * half, w[1])

    def place(s, low, high, b, top_row, count):
        size = count * cols
        col = lax.broadcasted_iota(jnp.int32, (size, d), 0) % cols
        left = jnp.broadcast_to(low[:, None, :], (count, cols, d)).reshape(size, d)
        right = jnp.broadcast_to(high[:, None, :], (count, cols, d)).reshape(size, d)
        minus = jnp.where(col == 0, left, pltpu.roll(s, 1, 0))
        plus = jnp.where(col == cols - 1, right, pltpu.roll(s, size - 1, 0))
        window = pl.ds(top_row * cols, size)
        shifted[0, b, window, :] = minus.astype(bf16)
        shifted[1, b, window, :] = s.astype(bf16)
        shifted[2, b, window, :] = plus.astype(bf16)

    for b in range(samples):
        for k, row in ((1, 0), (6, rows + 1)):
            at = base[k] + b * cols
            low, high = base[k - 1] + b, base[k + 1] + b
            place(hs[at : at + cols], hs[low : low + 1], hs[high : high + 1], b, row, 1)
    for c in range(chunks):
        b, part = divmod(c, per)
        at = b * rows + part * step
        low, high = base[3] + at, base[4] + at
        place(
            one_buf[pl.ds(c * chunk, chunk), :], hs[low : low + step], hs[high : high + step],
            b, 1 + part * step, step,
        )

    def body(c, carry):
        b = c // per
        part = c % per
        window = pl.ds(pl.multiple_of(c * chunk, chunk), chunk)
        flags = live_buf[pl.ds(pl.multiple_of(part * chunk, chunk), chunk), :]
        r = recv[window, :]
        total = jnp.zeros((chunk, d), f32)
        for k, (p, q) in enumerate(offsets):
            start = pl.multiple_of((part * step + 1 + p) * cols, cols)
            u = r + shifted[q + 1, b, pl.ds(start, chunk), :]
            z = mm(half_silu(u), w2h[0]).astype(bf16)
            on = jnp.broadcast_to(flags[:, k : k + 1], (chunk, LANES)).astype(bf16)
            on = jnp.concatenate([on] * (d // LANES), axis=1)
            total = total + (half_silu(z) * on).astype(f32)
        average = (total * 0.125).astype(bf16)
        avg_buf[window, :] = average
        one = x_buf[window, :] + mm(average, w[3])
        one_buf[window, :] = one
        small = chunk // 16
        pool_buf[pl.ds(pl.multiple_of(c * small, small), small), :] = (
            mm(pool_ref[...], one.astype(bf16)) * (1 / 16)
        ).astype(bf16)
        pltpu.make_async_copy(avg_buf.at[window], avg_hbm.at[window], avg_sems.at[c]).start()
        pltpu.make_async_copy(one_buf.at[window], one_hbm.at[window], one_sems.at[c]).start()
        return carry

    lax.fori_loop(0, chunks, body, 0)

    def small_pass(level, state, level_dims, pick, gather, send, full, hidden):
        _, n_rows, n_cols = level_dims
        padded = state.shape[0]
        xh = state.astype(bf16) * half
        s = mm(xh, w[4 * level + 1]).astype(bf16)
        full[pl.ds(0, padded), :] = s
        send[...] = mm(pick[...], s).astype(bf16)
        moves = exchange(level, send, full, {k: (k * EDGE, EDGE) for k in range(8)}, padded)
        w2h[level] = w[4 * level + 2] * half
        r = mm(xh, w[4 * level]) + bias_ref[level : level + 1, :] * 0.5
        for move in moves:
            move.wait()
        near = mm(gather[...], full[...])
        for k in range(8):
            u = r + near[k * padded : (k + 1) * padded]
            hidden[pl.ds(k * padded, padded), :] = half_silu(u).astype(bf16)
        message = half_silu(mm(hidden[...], w2h[level]))
        row = lax.broadcasted_iota(jnp.int32, (padded, d), 0) // n_cols % n_rows
        first = row == jnp.where(lat == 0, 0, -1)
        last = row == jnp.where(lat == lats - 1, n_rows - 1, -1)
        total = jnp.zeros((padded, d), f32)
        for k, (p, q) in enumerate(offsets):
            part = message[k * padded : (k + 1) * padded]
            if p:
                part = jnp.where(first if p < 0 else last, 0.0, part)
            total = total + part
        return state + mm((total * 0.125).astype(bf16), w[4 * level + 3])

    for load in loads[1:]:
        load.wait()
    mid_zero = mid_ref[...] + silu(mm(pool_buf[...], w[12]))
    mid_one = small_pass(1, mid_zero, mid_dims, pick_mid, gather_mid, mid_send, mid_full, mid_hidden)
    small = (mm(pool_mid[...], mid_one.astype(bf16)) * (1 / 16)).astype(bf16)
    coarse_zero = coarse_ref[...] + silu(mm(small, w[13]))
    coarse_one = small_pass(
        2, coarse_zero, coarse_dims, pick_coarse, gather_coarse, coarse_send, coarse_full, coarse_hidden
    )
    lifted = silu(mm(coarse_one.astype(bf16), w[14])).astype(bf16)
    mid_two = mid_one + mm(spread_mid[...], lifted)
    spread_ref[...] = silu(mm(mid_two.astype(bf16), w[15])).astype(bf16)

    def finish(c, carry):
        window = pl.ds(pl.multiple_of(c * chunk, chunk), chunk)
        pltpu.make_async_copy(avg_buf.at[window], avg_hbm.at[window], avg_sems.at[c]).wait()
        pltpu.make_async_copy(one_buf.at[window], one_hbm.at[window], one_sems.at[c]).wait()
        return carry

    lax.fori_loop(0, chunks, finish, 0)


def add_kernel(one_ref, spread_ref, table_ref, out_ref):
    out_ref[...] = one_ref[...] + mm(table_ref[...], spread_ref[...])


def local(
    fine_nodes, mid_nodes, coarse_nodes, edge_flags, proc_weights, bridge_weights, proc_biases
):
    samples, rows, cols, d = fine_nodes.shape
    mid_dims, coarse_dims = mid_nodes.shape[:3], coarse_nodes.shape[:3]
    step = 8
    chunk = step * cols
    total = samples * rows * cols
    chunks = total // chunk
    mid_count, coarse_count = int(np.prod(mid_dims)), int(np.prod(coarse_dims))
    coarse_padded = -(-coarse_count // 16) * 16
    pick_mid, gather_mid = small_tables(*mid_dims)
    pick_coarse, gather_coarse = small_tables(*coarse_dims)
    pool = pool_table(step, cols, chunk // 16)
    pool_mid = np.zeros((coarse_padded, mid_count), np.float32)
    each, few = mid_count // samples, coarse_count // samples
    for b in range(samples):
        pool_mid[b * few : (b + 1) * few, b * each : (b + 1) * each] = pool_table(*mid_dims[1:], few)
    place = np.zeros((8, cols, 8 * cols), np.float32)
    count = np.zeros((8 * cols, 8), np.float32)
    for k in range(8):
        place[k, np.arange(cols), k * cols + np.arange(cols)] = 1
        count[k * cols : (k + 1) * cols, k] = 1
    row_of = (np.arange(rows * cols)[:, None] // cols == np.arange(rows)[None, :])
    tables = [
        jnp.asarray(t, bf16) for t in (pool, place, row_of.astype(np.float32), count)
    ]
    levels = [
        pick_mid, gather_mid, pick_coarse, gather_coarse,
        jnp.asarray(pool_mid, bf16), jnp.asarray(pool_mid.T, bf16),
    ]
    coarse = jnp.pad(coarse_nodes.reshape(coarse_count, d), ((0, coarse_padded - coarse_count), (0, 0)))
    halo_rows = 2 * samples * (rows + cols) + 4 * EDGE
    vmem = pl.BlockSpec(memory_space=pltpu.VMEM)
    anywhere = pl.BlockSpec(memory_space=pl.ANY)
    dma = pltpu.SemaphoreType.DMA
    one, average, spread = pl.pallas_call(
        functools.partial(sweep_kernel, (samples, rows, cols, d, step, mid_dims, coarse_dims)),
        out_shape=(
            jax.ShapeDtypeStruct((total, d), f32),
            jax.ShapeDtypeStruct((total, d), bf16),
            jax.ShapeDtypeStruct((mid_count, d), bf16),
        ),
        in_specs=[anywhere, vmem, vmem, vmem, anywhere, anywhere, vmem] + [vmem] * 10,
        out_specs=(anywhere, anywhere, vmem),
        scratch_shapes=[
            pltpu.VMEM((total, d), bf16),
            pltpu.VMEM((3, samples, (rows + 2) * cols, d), bf16),
            pltpu.VMEM((total, d), f32),
            pltpu.VMEM((total, d), f32),
            pltpu.VMEM((total, d), bf16),
            pltpu.VMEM((16, d, d), bf16),
            pltpu.VMEM((3, d, d), bf16),
            pltpu.VMEM((rows * cols, 8), f32),
            pltpu.VMEM((mid_count, d), bf16),
            pltpu.VMEM((halo_rows, d), bf16),
            pltpu.VMEM((halo_rows, d), bf16),
            pltpu.VMEM((8 * EDGE, d), bf16),
            pltpu.VMEM((mid_count + 8 * EDGE, d), bf16),
            pltpu.VMEM((8 * EDGE, d), bf16),
            pltpu.VMEM((coarse_padded + 8 * EDGE, d), bf16),
            pltpu.VMEM((8 * mid_count, d), bf16),
            pltpu.VMEM((8 * coarse_padded, d), bf16),
            dma((chunks,)), dma((4,)), dma((chunks,)), dma((chunks,)), dma((24,)), dma((24,)),
        ],
        compiler_params=pltpu.CompilerParams(
            vmem_limit_bytes=60 << 20, collective_id=0, has_side_effects=True
        ),
        name="sweep",
    )(
        fine_nodes.reshape(total, d), mid_nodes.reshape(mid_count, d), coarse, edge_flags,
        proc_weights, bridge_weights, proc_biases, *tables, *levels,
    )
    block = pl.BlockSpec((chunk, d), lambda c: (c, 0))
    refined = pl.pallas_call(
        add_kernel,
        out_shape=jax.ShapeDtypeStruct((total, d), f32),
        grid=(chunks,),
        in_specs=[
            block,
            pl.BlockSpec((chunk // 16, d), lambda c: (c, 0)),
            pl.BlockSpec((chunk, chunk // 16), lambda c: (0, 0)),
        ],
        out_specs=block,
        name="add",
    )(one, spread, jnp.asarray(pool.T, bf16))
    return (refined.reshape(fine_nodes.shape), average.reshape(fine_nodes.shape))


def solution(mesh):
    placed = (
        P(None, "lat", "lon", None),
        P(None, "lat", "lon", None),
        P(None, "lat", "lon", None),
        P(None, "lat", "lon"),
        P(),
        P(),
        P(),
    )
    return jax.shard_map(
        local,
        mesh=mesh,
        in_specs=placed,
        out_specs=(P(None, "lat", "lon", None), P(None, "lat", "lon", None)),
        check_vma=False,
    )
```

```python
import functools

import jax
import jax.numpy as jnp
import numpy as np
from jax import lax
from jax.experimental import pallas as pl
from jax.experimental.pallas import tpu as pltpu
from jax.sharding import PartitionSpec as P

offsets = ((-1, -1), (-1, 0), (-1, 1), (0, -1), (0, 1), (1, -1), (1, 0), (1, 1))
bf16 = jnp.bfloat16
f32 = jnp.float32
MESH = pl.DeviceIdType.MESH
LANES = 128
EDGE = 16


def mm(a, b):
    return jnp.dot(a, b, preferred_element_type=f32)


def half_silu(u):
    return u * jnp.tanh(u) + u


def silu(x):
    return half_silu(x * 0.5)


def edge_of(step, count):
    if step == 0:
        return list(range(count))
    return [count - 1] if step < 0 else [0]


def small_tables(samples, rows, cols):
    nodes = samples * rows * cols
    padded = -(-nodes // 16) * 16
    pick = np.zeros((8 * EDGE, padded), np.float32)
    slot = {}
    for k, (p, q) in enumerate(offsets):
        e = 0
        for b in range(samples):
            for i in edge_of(p, rows):
                for j in edge_of(q, cols):
                    pick[k * EDGE + e, (b * rows + i) * cols + j] = 1
                    slot[k, b, i, j] = padded + k * EDGE + e
                    e += 1
        assert e <= EDGE
    gather = np.zeros((8, padded, padded + 8 * EDGE), np.float32)
    for k, (p, q) in enumerate(offsets):
        for b in range(samples):
            for i in range(rows):
                for j in range(cols):
                    a, c = i + p, j + q
                    over = (-1 if a < 0 else int(a >= rows), -1 if c < 0 else int(c >= cols))
                    if over == (0, 0):
                        source = (b * rows + a) * cols + c
                    else:
                        source = slot[offsets.index(over), b, a % rows, c % cols]
                    gather[k, (b * rows + i) * cols + j, source] = 1
    return jnp.asarray(pick, bf16), jnp.asarray(gather.reshape(8 * padded, -1), bf16)


def pool_table(rows, cols, out_rows):
    n = np.arange(rows * cols)
    parent = (n // cols // 4) * (cols // 4) + (n % cols) // 4
    return (parent[None, :] == np.arange(out_rows)[:, None]).astype(np.float32)


def sweep_kernel(
    dims,
    x_hbm, mid_ref, coarse_ref, flag_ref, proc_hbm, bridge_hbm, bias_ref,
    pool_ref, place_ref, row_ref, count_ref,
    pick_mid, gather_mid, pick_coarse, gather_coarse, pool_mid, spread_mid,
    one_hbm, avg_hbm, spread_ref,
    recv, shifted, x_buf, one_buf, avg_buf, w, w2h, live_buf, pool_buf,
    out_buf, halo, mid_send, mid_full, coarse_send, coarse_full, mid_hidden, coarse_hidden,
    x_sems, w_sems, one_sems, avg_sems, send_sems, recv_sems,
):
    samples, rows, cols, d, step, mid_dims, coarse_dims = dims
    per = rows // step
    chunk = step * cols
    chunks = samples * per
    lat, lon = lax.axis_index("lat"), lax.axis_index("lon")
    lats, lons = lax.axis_size("lat"), lax.axis_size("lon")
    half = jnp.asarray(0.5, bf16)

    def target(k):
        p, q = offsets[k]
        return (lax.rem(lat - p + lats, lats), lax.rem(lon - q + lons, lons))

    barrier = pltpu.get_barrier_semaphore()
    for k in range(8):
        pl.semaphore_signal(barrier, inc=1, device_id=target(k), device_id_type=MESH)
    copies = [
        pltpu.make_async_copy(x_hbm.at[pl.ds(c * chunk, chunk)], x_buf.at[pl.ds(c * chunk, chunk)], x_sems.at[c])
        for c in range(chunks)
    ]
    loads = [pltpu.make_async_copy(proc_hbm.at[0], w.at[pl.ds(0, 4)], w_sems.at[0])]
    loads += [pltpu.make_async_copy(proc_hbm.at[1], w.at[pl.ds(4, 4)], w_sems.at[1])]
    loads += [pltpu.make_async_copy(proc_hbm.at[2], w.at[pl.ds(8, 4)], w_sems.at[2])]
    loads += [pltpu.make_async_copy(bridge_hbm, w.at[pl.ds(12, 4)], w_sems.at[3])]
    for copy in copies + loads:
        copy.start()

    table = jnp.zeros((rows, 8 * cols), f32)
    for k in range(8):
        table = table + mm(flag_ref[k].astype(bf16), place_ref[k])
    spread_flags = mm(row_ref[...], table.astype(bf16))
    node = lax.broadcasted_iota(jnp.int32, spread_flags.shape, 0)
    lane = lax.broadcasted_iota(jnp.int32, spread_flags.shape, 1)
    own = jnp.where(node % cols == lane % cols, spread_flags, 0.0).astype(bf16)
    live = mm(own, count_ref[...])
    node = lax.broadcasted_iota(jnp.int32, live.shape, 0) // cols
    lane = lax.broadcasted_iota(jnp.int32, live.shape, 1)
    top = jnp.where(lat == 0, 0, -1)
    bottom = jnp.where(lat == lats - 1, rows - 1, -1)
    live_buf[...] = jnp.where(
        ((lane < 3) & (node == top)) | ((lane > 4) & (node == bottom)), 0.0, live
    )

    for copy in copies:
        copy.wait()
    base = {1: 0, 6: samples * cols, 3: 2 * samples * cols, 4: 2 * samples * cols + samples * rows}
    size = {1: samples * cols, 6: samples * cols, 3: samples * rows, 4: samples * rows}
    corner = 2 * samples * (cols + rows)
    for n, k in enumerate((0, 2, 5, 7)):
        base[k], size[k] = corner + n * EDGE, EDGE
    per_sample = rows * cols
    grid_buf = x_buf.reshape(samples * rows, cols, d)
    row16 = lax.broadcasted_iota(jnp.int32, (EDGE, d), 0)
    for k, (p, q) in enumerate(offsets):
        i, j = edge_of(p, rows)[0], edge_of(q, cols)[0]
        if p == 0:
            out_buf[pl.ds(base[k], size[k]), :] = grid_buf[:, j, :].astype(bf16)
        elif q == 0:
            for b in range(samples):
                out_buf[pl.ds(base[k] + b * cols, cols), :] = x_buf[
                    pl.ds(b * per_sample + i * cols, cols), :
                ].astype(bf16)
        else:
            value = jnp.zeros((EDGE, d), f32)
            for b in range(samples):
                at = b * per_sample + i * cols + j
                value = jnp.where(row16 == b, jnp.broadcast_to(x_buf[at : at + 1, :], (EDGE, d)), value)
            out_buf[pl.ds(base[k], EDGE), :] = value.astype(bf16)
    pl.semaphore_wait(barrier, 8)

    def exchange(level, source, dest, spans, shift):
        sends = []
        for k in range(8):
            at, count = spans[k]
            sends.append(
                pltpu.make_async_remote_copy(
                    src_ref=source.at[pl.ds(at, count)],
                    dst_ref=dest.at[pl.ds(shift + at, count)],
                    send_sem=send_sems.at[level * 8 + k],
                    recv_sem=recv_sems.at[level * 8 + k],
                    device_id=target(k),
                    device_id_type=MESH,
                )
            )
        for send in sends:
            send.start()
        return sends

    sends = exchange(0, out_buf, halo, {k: (base[k], size[k]) for k in range(8)}, 0)

    loads[0].wait()
    w2h[0] = w[2] * half
    bias = bias_ref[0:1, :] * 0.5

    def project_body(c, carry):
        window = pl.ds(pl.multiple_of(c * chunk, chunk), chunk)
        xh = x_buf[window, :].astype(bf16) * half
        recv[window, :] = (mm(xh, w[0]) + bias).astype(bf16)
        one_buf[window, :] = mm(xh, w[1])
        return carry

    lax.fori_loop(0, chunks, project_body, 0)
    for send in sends:
        send.wait()
    hs = mm(halo[...] * half, w[1])

    def place(s, low, high, b, top_row, count):
        size = count * cols
        col = lax.broadcasted_iota(jnp.int32, (size, d), 0) % cols
        left = jnp.broadcast_to(low[:, None, :], (count, cols, d)).reshape(size, d)
        right = jnp.broadcast_to(high[:, None, :], (count, cols, d)).reshape(size, d)
        minus = jnp.where(col == 0, left, pltpu.roll(s, 1, 0))
        plus = jnp.where(col == cols - 1, right, pltpu.roll(s, size - 1, 0))
        window = pl.ds(top_row * cols, size)
        shifted[0, b, window, :] = minus.astype(bf16)
        shifted[1, b, window, :] = s.astype(bf16)
        shifted[2, b, window, :] = plus.astype(bf16)

    for b in range(samples):
        for k, row in ((1, 0), (6, rows + 1)):
            at = base[k] + b * cols
            low, high = base[k - 1] + b, base[k + 1] + b
            place(hs[at : at + cols], hs[low : low + 1], hs[high : high + 1], b, row, 1)
    for c in range(chunks):
        b, part = divmod(c, per)
        at = b * rows + part * step
        low, high = base[3] + at, base[4] + at
        place(
            one_buf[pl.ds(c * chunk, chunk), :], hs[low : low + step], hs[high : high + step],
            b, 1 + part * step, step,
        )

    def body(c, carry):
        b = c // per
        part = c % per
        window = pl.ds(pl.multiple_of(c * chunk, chunk), chunk)
        flags = live_buf[pl.ds(pl.multiple_of(part * chunk, chunk), chunk), :]
        r = recv[window, :]
        total = jnp.zeros((chunk, d), f32)
        for k, (p, q) in enumerate(offsets):
            start = pl.multiple_of((part * step + 1 + p) * cols, cols)
            u = r + shifted[q + 1, b, pl.ds(start, chunk), :]
            z = mm(half_silu(u), w2h[0]).astype(bf16)
            on = jnp.broadcast_to(flags[:, k : k + 1], (chunk, LANES)).astype(bf16)
            on = jnp.concatenate([on] * (d // LANES), axis=1)
            total = total + (half_silu(z) * on).astype(f32)
        average = (total * 0.125).astype(bf16)
        avg_buf[window, :] = average
        one = x_buf[window, :] + mm(average, w[3])
        one_buf[window, :] = one
        small = chunk // 16
        pool_buf[pl.ds(pl.multiple_of(c * small, small), small), :] = (
            mm(pool_ref[...], one.astype(bf16)) * (1 / 16)
        ).astype(bf16)
        pltpu.make_async_copy(avg_buf.at[window], avg_hbm.at[window], avg_sems.at[c]).start()
        pltpu.make_async_copy(one_buf.at[window], one_hbm.at[window], one_sems.at[c]).start()
        return carry

    lax.fori_loop(0, chunks, body, 0)

    def small_pass(level, state, level_dims, pick, gather, send, full, hidden):
        _, n_rows, n_cols = level_dims
        padded = state.shape[0]
        xh = state.astype(bf16) * half
        s = mm(xh, w[4 * level + 1]).astype(bf16)
        full[pl.ds(0, padded), :] = s
        send[...] = mm(pick[...], s).astype(bf16)
        moves = exchange(level, send, full, {k: (k * EDGE, EDGE) for k in range(8)}, padded)
        w2h[level] = w[4 * level + 2] * half
        r = mm(xh, w[4 * level]) + bias_ref[level : level + 1, :] * 0.5
        for move in moves:
            move.wait()
        near = mm(gather[...], full[...])
        for k in range(8):
            u = r + near[k * padded : (k + 1) * padded]
            hidden[pl.ds(k * padded, padded), :] = half_silu(u).astype(bf16)
        message = half_silu(mm(hidden[...], w2h[level]))
        row = lax.broadcasted_iota(jnp.int32, (padded, d), 0) // n_cols % n_rows
        first = row == jnp.where(lat == 0, 0, -1)
        last = row == jnp.where(lat == lats - 1, n_rows - 1, -1)
        total = jnp.zeros((padded, d), f32)
        for k, (p, q) in enumerate(offsets):
            part = message[k * padded : (k + 1) * padded]
            if p:
                part = jnp.where(first if p < 0 else last, 0.0, part)
            total = total + part
        return state + mm((total * 0.125).astype(bf16), w[4 * level + 3])

    for load in loads[1:]:
        load.wait()
    mid_zero = mid_ref[...] + silu(mm(pool_buf[...], w[12]))
    mid_one = small_pass(1, mid_zero, mid_dims, pick_mid, gather_mid, mid_send, mid_full, mid_hidden)
    small = (mm(pool_mid[...], mid_one.astype(bf16)) * (1 / 16)).astype(bf16)
    coarse_zero = silu(mm(small, w[13]))
    row = lax.broadcasted_iota(jnp.int32, coarse_zero.shape, 0)
    nodes = jnp.zeros(coarse_zero.shape, f32)
    _, coarse_rows, coarse_cols = coarse_dims
    for n in range(int(np.prod(coarse_dims))):
        b, i = divmod(n // coarse_cols, coarse_rows)
        j = n % coarse_cols
        nodes = jnp.where(row == n, jnp.broadcast_to(coarse_ref[b, i, j : j + 1, :], nodes.shape), nodes)
    coarse_zero = coarse_zero + nodes
    coarse_one = small_pass(
        2, coarse_zero, coarse_dims, pick_coarse, gather_coarse, coarse_send, coarse_full, coarse_hidden
    )
    lifted = silu(mm(coarse_one.astype(bf16), w[14])).astype(bf16)
    mid_two = mid_one + mm(spread_mid[...], lifted)
    spread_ref[...] = silu(mm(mid_two.astype(bf16), w[15])).astype(bf16)

    def finish(c, carry):
        window = pl.ds(pl.multiple_of(c * chunk, chunk), chunk)
        pltpu.make_async_copy(avg_buf.at[window], avg_hbm.at[window], avg_sems.at[c]).wait()
        pltpu.make_async_copy(one_buf.at[window], one_hbm.at[window], one_sems.at[c]).wait()
        return carry

    lax.fori_loop(0, chunks, finish, 0)


def add_kernel(one_ref, spread_ref, table_ref, out_ref):
    out_ref[...] = one_ref[...] + mm(table_ref[...], spread_ref[...])


def local(
    fine_nodes, mid_nodes, coarse_nodes, edge_flags, proc_weights, bridge_weights, proc_biases
):
    samples, rows, cols, d = fine_nodes.shape
    mid_dims, coarse_dims = mid_nodes.shape[:3], coarse_nodes.shape[:3]
    step = 16
    chunk = step * cols
    total = samples * rows * cols
    chunks = total // chunk
    mid_count, coarse_count = int(np.prod(mid_dims)), int(np.prod(coarse_dims))
    coarse_padded = -(-coarse_count // 16) * 16
    pick_mid, gather_mid = small_tables(*mid_dims)
    pick_coarse, gather_coarse = small_tables(*coarse_dims)
    pool = pool_table(step, cols, chunk // 16)
    pool_mid = np.zeros((coarse_padded, mid_count), np.float32)
    each, few = mid_count // samples, coarse_count // samples
    for b in range(samples):
        pool_mid[b * few : (b + 1) * few, b * each : (b + 1) * each] = pool_table(*mid_dims[1:], few)
    place = np.zeros((8, cols, 8 * cols), np.float32)
    count = np.zeros((8 * cols, 8), np.float32)
    for k in range(8):
        place[k, np.arange(cols), k * cols + np.arange(cols)] = 1
        count[k * cols : (k + 1) * cols, k] = 1
    row_of = (np.arange(rows * cols)[:, None] // cols == np.arange(rows)[None, :])
    tables = [
        jnp.asarray(t, bf16) for t in (pool, place, row_of.astype(np.float32), count)
    ]
    levels = [
        pick_mid, gather_mid, pick_coarse, gather_coarse,
        jnp.asarray(pool_mid, bf16), jnp.asarray(pool_mid.T, bf16),
    ]
    halo_rows = 2 * samples * (rows + cols) + 4 * EDGE
    vmem = pl.BlockSpec(memory_space=pltpu.VMEM)
    anywhere = pl.BlockSpec(memory_space=pl.ANY)
    dma = pltpu.SemaphoreType.DMA
    one, average, spread = pl.pallas_call(
        functools.partial(sweep_kernel, (samples, rows, cols, d, step, mid_dims, coarse_dims)),
        out_shape=(
            jax.ShapeDtypeStruct((total, d), f32),
            jax.ShapeDtypeStruct((total, d), bf16),
            jax.ShapeDtypeStruct((mid_count, d), bf16),
        ),
        in_specs=[anywhere, vmem, vmem, vmem, anywhere, anywhere, vmem] + [vmem] * 10,
        out_specs=(anywhere, anywhere, vmem),
        scratch_shapes=[
            pltpu.VMEM((total, d), bf16),
            pltpu.VMEM((3, samples, (rows + 2) * cols, d), bf16),
            pltpu.VMEM((total, d), f32),
            pltpu.VMEM((total, d), f32),
            pltpu.VMEM((total, d), bf16),
            pltpu.VMEM((16, d, d), bf16),
            pltpu.VMEM((3, d, d), bf16),
            pltpu.VMEM((rows * cols, 8), f32),
            pltpu.VMEM((mid_count, d), bf16),
            pltpu.VMEM((halo_rows, d), bf16),
            pltpu.VMEM((halo_rows, d), bf16),
            pltpu.VMEM((8 * EDGE, d), bf16),
            pltpu.VMEM((mid_count + 8 * EDGE, d), bf16),
            pltpu.VMEM((8 * EDGE, d), bf16),
            pltpu.VMEM((coarse_padded + 8 * EDGE, d), bf16),
            pltpu.VMEM((8 * mid_count, d), bf16),
            pltpu.VMEM((8 * coarse_padded, d), bf16),
            dma((chunks,)), dma((4,)), dma((chunks,)), dma((chunks,)), dma((24,)), dma((24,)),
        ],
        compiler_params=pltpu.CompilerParams(
            vmem_limit_bytes=60 << 20, collective_id=0, has_side_effects=True
        ),
        name="sweep",
    )(
        fine_nodes.reshape(total, d), mid_nodes.reshape(mid_count, d), coarse_nodes, edge_flags,
        proc_weights, bridge_weights, proc_biases, *tables, *levels,
    )
    block = pl.BlockSpec((chunk, d), lambda c: (c, 0))
    refined = pl.pallas_call(
        add_kernel,
        out_shape=jax.ShapeDtypeStruct((total, d), f32),
        grid=(chunks,),
        in_specs=[
            block,
            pl.BlockSpec((chunk // 16, d), lambda c: (c, 0)),
            pl.BlockSpec((chunk, chunk // 16), lambda c: (0, 0)),
        ],
        out_specs=block,
        name="add",
    )(one, spread, jnp.asarray(pool.T, bf16))
    return (refined.reshape(fine_nodes.shape), average.reshape(fine_nodes.shape))


def solution(mesh):
    placed = (
        P(None, "lat", "lon", None),
        P(None, "lat", "lon", None),
        P(None, "lat", "lon", None),
        P(None, "lat", "lon"),
        P(),
        P(),
        P(),
    )
    return jax.shard_map(
        local,
        mesh=mesh,
        in_specs=placed,
        out_specs=(P(None, "lat", "lon", None), P(None, "lat", "lon", None)),
        check_vma=False,
    )
```

```python
import functools

import jax
import jax.numpy as jnp
import numpy as np
from jax import lax
from jax.experimental import pallas as pl
from jax.experimental.pallas import tpu as pltpu
from jax.sharding import PartitionSpec as P

offsets = ((-1, -1), (-1, 0), (-1, 1), (0, -1), (0, 1), (1, -1), (1, 0), (1, 1))
bf16 = jnp.bfloat16
f32 = jnp.float32
MESH = pl.DeviceIdType.MESH
LANES = 128
EDGE = 16


def mm(a, b):
    return jnp.dot(a, b, preferred_element_type=f32)


def half_silu(u):
    return u * jnp.tanh(u) + u


def silu(x):
    return half_silu(x * 0.5)


def edge_of(step, count):
    if step == 0:
        return list(range(count))
    return [count - 1] if step < 0 else [0]


def small_tables(samples, rows, cols):
    nodes = samples * rows * cols
    padded = -(-nodes // 16) * 16
    pick = np.zeros((8 * EDGE, padded), np.float32)
    slot = {}
    for k, (p, q) in enumerate(offsets):
        e = 0
        for b in range(samples):
            for i in edge_of(p, rows):
                for j in edge_of(q, cols):
                    pick[k * EDGE + e, (b * rows + i) * cols + j] = 1
                    slot[k, b, i, j] = padded + k * EDGE + e
                    e += 1
        assert e <= EDGE
    gather = np.zeros((8, padded, padded + 8 * EDGE), np.float32)
    for k, (p, q) in enumerate(offsets):
        for b in range(samples):
            for i in range(rows):
                for j in range(cols):
                    a, c = i + p, j + q
                    over = (-1 if a < 0 else int(a >= rows), -1 if c < 0 else int(c >= cols))
                    if over == (0, 0):
                        source = (b * rows + a) * cols + c
                    else:
                        source = slot[offsets.index(over), b, a % rows, c % cols]
                    gather[k, (b * rows + i) * cols + j, source] = 1
    return jnp.asarray(pick, bf16), jnp.asarray(gather.reshape(8 * padded, -1), bf16)


def pool_table(rows, cols, out_rows):
    n = np.arange(rows * cols)
    parent = (n // cols // 4) * (cols // 4) + (n % cols) // 4
    return (parent[None, :] == np.arange(out_rows)[:, None]).astype(np.float32)


def sweep_kernel(
    dims,
    x_hbm, mid_ref, coarse_ref, flag_ref, proc_hbm, bridge_hbm, bias_ref,
    pool_ref, place_ref, row_ref, count_ref,
    pick_mid, gather_mid, pick_coarse, gather_coarse, pool_mid, spread_mid,
    one_hbm, avg_hbm, spread_ref,
    recv, shifted, x_buf, one_buf, avg_buf, w, w2h, live_buf, pool_buf,
    out_buf, halo, mid_send, mid_full, coarse_send, coarse_full, mid_hidden, coarse_hidden,
    x_sems, w_sems, one_sems, avg_sems, send_sems, recv_sems,
):
    samples, rows, cols, d, step, mid_dims, coarse_dims = dims
    per = rows // step
    chunk = step * cols
    chunks = samples * per
    lat, lon = lax.axis_index("lat"), lax.axis_index("lon")
    lats, lons = lax.axis_size("lat"), lax.axis_size("lon")
    half = jnp.asarray(0.5, bf16)

    def target(k):
        p, q = offsets[k]
        return (lax.rem(lat - p + lats, lats), lax.rem(lon - q + lons, lons))

    barrier = pltpu.get_barrier_semaphore()
    for k in range(8):
        pl.semaphore_signal(barrier, inc=1, device_id=target(k), device_id_type=MESH)
    copies = [
        pltpu.make_async_copy(x_hbm.at[pl.ds(c * chunk, chunk)], x_buf.at[pl.ds(c * chunk, chunk)], x_sems.at[c])
        for c in range(chunks)
    ]
    loads = [pltpu.make_async_copy(proc_hbm.at[0], w.at[pl.ds(0, 4)], w_sems.at[0])]
    loads += [pltpu.make_async_copy(proc_hbm.at[1], w.at[pl.ds(4, 4)], w_sems.at[1])]
    loads += [pltpu.make_async_copy(proc_hbm.at[2], w.at[pl.ds(8, 4)], w_sems.at[2])]
    loads += [pltpu.make_async_copy(bridge_hbm, w.at[pl.ds(12, 4)], w_sems.at[3])]
    for copy in copies + loads:
        copy.start()

    table = jnp.zeros((rows, 8 * cols), f32)
    for k in range(8):
        table = table + mm(flag_ref[k].astype(bf16), place_ref[k])
    spread_flags = mm(row_ref[...], table.astype(bf16))
    node = lax.broadcasted_iota(jnp.int32, spread_flags.shape, 0)
    lane = lax.broadcasted_iota(jnp.int32, spread_flags.shape, 1)
    own = jnp.where(node % cols == lane % cols, spread_flags, 0.0).astype(bf16)
    live = mm(own, count_ref[...])
    node = lax.broadcasted_iota(jnp.int32, live.shape, 0) // cols
    lane = lax.broadcasted_iota(jnp.int32, live.shape, 1)
    top = jnp.where(lat == 0, 0, -1)
    bottom = jnp.where(lat == lats - 1, rows - 1, -1)
    live_buf[...] = jnp.where(
        ((lane < 3) & (node == top)) | ((lane > 4) & (node == bottom)), 0.0, live
    )

    for copy in copies:
        copy.wait()
    base = {1: 0, 6: samples * cols, 3: 2 * samples * cols, 4: 2 * samples * cols + samples * rows}
    size = {1: samples * cols, 6: samples * cols, 3: samples * rows, 4: samples * rows}
    corner = 2 * samples * (cols + rows)
    for n, k in enumerate((0, 2, 5, 7)):
        base[k], size[k] = corner + n * EDGE, EDGE
    per_sample = rows * cols
    grid_buf = x_buf.reshape(samples * rows, cols, d)
    row16 = lax.broadcasted_iota(jnp.int32, (EDGE, d), 0)
    for k, (p, q) in enumerate(offsets):
        i, j = edge_of(p, rows)[0], edge_of(q, cols)[0]
        if p == 0:
            out_buf[pl.ds(base[k], size[k]), :] = grid_buf[:, j, :].astype(bf16)
        elif q == 0:
            for b in range(samples):
                out_buf[pl.ds(base[k] + b * cols, cols), :] = x_buf[
                    pl.ds(b * per_sample + i * cols, cols), :
                ].astype(bf16)
        else:
            value = jnp.zeros((EDGE, d), f32)
            for b in range(samples):
                at = b * per_sample + i * cols + j
                value = jnp.where(row16 == b, jnp.broadcast_to(x_buf[at : at + 1, :], (EDGE, d)), value)
            out_buf[pl.ds(base[k], EDGE), :] = value.astype(bf16)
    pl.semaphore_wait(barrier, 8)

    def exchange(level, source, dest, spans, shift):
        sends = []
        for k in range(8):
            at, count = spans[k]
            sends.append(
                pltpu.make_async_remote_copy(
                    src_ref=source.at[pl.ds(at, count)],
                    dst_ref=dest.at[pl.ds(shift + at, count)],
                    send_sem=send_sems.at[level * 8 + k],
                    recv_sem=recv_sems.at[level * 8 + k],
                    device_id=target(k),
                    device_id_type=MESH,
                )
            )
        for send in sends:
            send.start()
        return sends

    sends = exchange(0, out_buf, halo, {k: (base[k], size[k]) for k in range(8)}, 0)

    loads[0].wait()
    w2h[0] = w[2] * half
    bias = bias_ref[0:1, :] * 0.5

    def project_body(c, carry):
        window = pl.ds(pl.multiple_of(c * chunk, chunk), chunk)
        xh = x_buf[window, :].astype(bf16) * half
        recv[window, :] = (mm(xh, w[0]) + bias).astype(bf16)
        one_buf[window, :] = mm(xh, w[1])
        return carry

    lax.fori_loop(0, chunks, project_body, 0)
    for send in sends:
        send.wait()
    hs = mm(halo[...] * half, w[1])

    def place(s, low, high, b, top_row, count):
        size = count * cols
        col = lax.broadcasted_iota(jnp.int32, (size, d), 0) % cols
        left = jnp.broadcast_to(low[:, None, :], (count, cols, d)).reshape(size, d)
        right = jnp.broadcast_to(high[:, None, :], (count, cols, d)).reshape(size, d)
        minus = jnp.where(col == 0, left, pltpu.roll(s, 1, 0))
        plus = jnp.where(col == cols - 1, right, pltpu.roll(s, size - 1, 0))
        window = pl.ds(top_row * cols, size)
        shifted[0, b, window, :] = minus.astype(bf16)
        shifted[1, b, window, :] = s.astype(bf16)
        shifted[2, b, window, :] = plus.astype(bf16)

    for b in range(samples):
        for k, row in ((1, 0), (6, rows + 1)):
            at = base[k] + b * cols
            low, high = base[k - 1] + b, base[k + 1] + b
            place(hs[at : at + cols], hs[low : low + 1], hs[high : high + 1], b, row, 1)
    for c in range(chunks):
        b, part = divmod(c, per)
        at = b * rows + part * step
        low, high = base[3] + at, base[4] + at
        place(
            one_buf[pl.ds(c * chunk, chunk), :], hs[low : low + step], hs[high : high + step],
            b, 1 + part * step, step,
        )

    def body(c, carry):
        b = c // per
        part = c % per
        window = pl.ds(pl.multiple_of(c * chunk, chunk), chunk)
        flags = live_buf[pl.ds(pl.multiple_of(part * chunk, chunk), chunk), :]
        r = recv[window, :]
        total = jnp.zeros((chunk, d), f32)
        for k, (p, q) in enumerate(offsets):
            start = pl.multiple_of((part * step + 1 + p) * cols, cols)
            u = r + shifted[q + 1, b, pl.ds(start, chunk), :]
            z = mm(half_silu(u), w2h[0]).astype(bf16)
            on = jnp.broadcast_to(flags[:, k : k + 1], (chunk, LANES)).astype(bf16)
            on = jnp.concatenate([on] * (d // LANES), axis=1)
            total = total + (half_silu(z) * on).astype(f32)
        average = (total * 0.125).astype(bf16)
        avg_buf[window, :] = average
        one = x_buf[window, :] + mm(average, w[3])
        one_buf[window, :] = one
        small = chunk // 16
        pool_buf[pl.ds(pl.multiple_of(c * small, small), small), :] = (
            mm(pool_ref[...], one.astype(bf16)) * (1 / 16)
        ).astype(bf16)
        pltpu.make_async_copy(avg_buf.at[window], avg_hbm.at[window], avg_sems.at[c]).start()
        pltpu.make_async_copy(one_buf.at[window], one_hbm.at[window], one_sems.at[c]).start()
        return carry

    lax.fori_loop(0, chunks, body, 0)

    def small_pass(level, state, level_dims, pick, gather, send, full, hidden):
        _, n_rows, n_cols = level_dims
        padded = state.shape[0]
        xh = state.astype(bf16) * half
        s = mm(xh, w[4 * level + 1]).astype(bf16)
        full[pl.ds(0, padded), :] = s
        send[...] = mm(pick[...], s).astype(bf16)
        moves = exchange(level, send, full, {k: (k * EDGE, EDGE) for k in range(8)}, padded)
        w2h[level] = w[4 * level + 2] * half
        r = mm(xh, w[4 * level]) + bias_ref[level : level + 1, :] * 0.5
        for move in moves:
            move.wait()
        near = mm(gather[...], full[...])
        for k in range(8):
            u = r + near[k * padded : (k + 1) * padded]
            hidden[pl.ds(k * padded, padded), :] = half_silu(u).astype(bf16)
        message = half_silu(mm(hidden[...], w2h[level]))
        row = lax.broadcasted_iota(jnp.int32, (padded, d), 0) // n_cols % n_rows
        first = row == jnp.where(lat == 0, 0, -1)
        last = row == jnp.where(lat == lats - 1, n_rows - 1, -1)
        total = jnp.zeros((padded, d), f32)
        for k, (p, q) in enumerate(offsets):
            part = message[k * padded : (k + 1) * padded]
            if p:
                part = jnp.where(first if p < 0 else last, 0.0, part)
            total = total + part
        return state + mm((total * 0.125).astype(bf16), w[4 * level + 3])

    for load in loads[1:]:
        load.wait()
    mid_zero = mid_ref[...] + silu(mm(pool_buf[...], w[12]))
    mid_one = small_pass(1, mid_zero, mid_dims, pick_mid, gather_mid, mid_send, mid_full, mid_hidden)
    small = (mm(pool_mid[...], mid_one.astype(bf16)) * (1 / 16)).astype(bf16)
    coarse_zero = silu(mm(small, w[13]))
    row = lax.broadcasted_iota(jnp.int32, coarse_zero.shape, 0)
    nodes = jnp.zeros(coarse_zero.shape, f32)
    _, coarse_rows, coarse_cols = coarse_dims
    for n in range(int(np.prod(coarse_dims))):
        b, i = divmod(n // coarse_cols, coarse_rows)
        j = n % coarse_cols
        nodes = jnp.where(row == n, jnp.broadcast_to(coarse_ref[b, i, j : j + 1, :], nodes.shape), nodes)
    coarse_zero = coarse_zero + nodes
    coarse_one = small_pass(
        2, coarse_zero, coarse_dims, pick_coarse, gather_coarse, coarse_send, coarse_full, coarse_hidden
    )
    lifted = silu(mm(coarse_one.astype(bf16), w[14])).astype(bf16)
    mid_two = mid_one + mm(spread_mid[...], lifted)
    spread_ref[...] = silu(mm(mid_two.astype(bf16), w[15])).astype(bf16)

    def finish(c, carry):
        window = pl.ds(pl.multiple_of(c * chunk, chunk), chunk)
        pltpu.make_async_copy(avg_buf.at[window], avg_hbm.at[window], avg_sems.at[c]).wait()
        pltpu.make_async_copy(one_buf.at[window], one_hbm.at[window], one_sems.at[c]).wait()
        return carry

    lax.fori_loop(0, chunks, finish, 0)


def add_kernel(one_hbm, spread_ref, table_ref, out_hbm, buf, in_sems, out_sems):
    chunk, small = table_ref.shape
    chunks = buf.shape[0] // chunk
    windows = [pl.ds(c * chunk, chunk) for c in range(chunks)]
    loads = [
        pltpu.make_async_copy(one_hbm.at[w], buf.at[w], in_sems.at[c]) for c, w in enumerate(windows)
    ]
    stores = [
        pltpu.make_async_copy(buf.at[w], out_hbm.at[w], out_sems.at[c]) for c, w in enumerate(windows)
    ]
    for load in loads:
        load.start()
    for c, w in enumerate(windows):
        term = mm(table_ref[...], spread_ref[c * small : (c + 1) * small, :])
        loads[c].wait()
        buf[w, :] = buf[w, :] + term
        stores[c].start()
    for store in stores:
        store.wait()


def local(
    fine_nodes, mid_nodes, coarse_nodes, edge_flags, proc_weights, bridge_weights, proc_biases
):
    samples, rows, cols, d = fine_nodes.shape
    mid_dims, coarse_dims = mid_nodes.shape[:3], coarse_nodes.shape[:3]
    step = 16
    chunk = step * cols
    total = samples * rows * cols
    chunks = total // chunk
    mid_count, coarse_count = int(np.prod(mid_dims)), int(np.prod(coarse_dims))
    coarse_padded = -(-coarse_count // 16) * 16
    pick_mid, gather_mid = small_tables(*mid_dims)
    pick_coarse, gather_coarse = small_tables(*coarse_dims)
    pool = pool_table(step, cols, chunk // 16)
    pool_mid = np.zeros((coarse_padded, mid_count), np.float32)
    each, few = mid_count // samples, coarse_count // samples
    for b in range(samples):
        pool_mid[b * few : (b + 1) * few, b * each : (b + 1) * each] = pool_table(*mid_dims[1:], few)
    place = np.zeros((8, cols, 8 * cols), np.float32)
    count = np.zeros((8 * cols, 8), np.float32)
    for k in range(8):
        place[k, np.arange(cols), k * cols + np.arange(cols)] = 1
        count[k * cols : (k + 1) * cols, k] = 1
    row_of = (np.arange(rows * cols)[:, None] // cols == np.arange(rows)[None, :])
    tables = [
        jnp.asarray(t, bf16) for t in (pool, place, row_of.astype(np.float32), count)
    ]
    levels = [
        pick_mid, gather_mid, pick_coarse, gather_coarse,
        jnp.asarray(pool_mid, bf16), jnp.asarray(pool_mid.T, bf16),
    ]
    halo_rows = 2 * samples * (rows + cols) + 4 * EDGE
    vmem = pl.BlockSpec(memory_space=pltpu.VMEM)
    anywhere = pl.BlockSpec(memory_space=pl.ANY)
    dma = pltpu.SemaphoreType.DMA
    one, average, spread = pl.pallas_call(
        functools.partial(sweep_kernel, (samples, rows, cols, d, step, mid_dims, coarse_dims)),
        out_shape=(
            jax.ShapeDtypeStruct((total, d), f32),
            jax.ShapeDtypeStruct((total, d), bf16),
            jax.ShapeDtypeStruct((mid_count, d), bf16),
        ),
        in_specs=[anywhere, vmem, vmem, vmem, anywhere, anywhere, vmem] + [vmem] * 10,
        out_specs=(anywhere, anywhere, vmem),
        scratch_shapes=[
            pltpu.VMEM((total, d), bf16),
            pltpu.VMEM((3, samples, (rows + 2) * cols, d), bf16),
            pltpu.VMEM((total, d), f32),
            pltpu.VMEM((total, d), f32),
            pltpu.VMEM((total, d), bf16),
            pltpu.VMEM((16, d, d), bf16),
            pltpu.VMEM((3, d, d), bf16),
            pltpu.VMEM((rows * cols, 8), f32),
            pltpu.VMEM((mid_count, d), bf16),
            pltpu.VMEM((halo_rows, d), bf16),
            pltpu.VMEM((halo_rows, d), bf16),
            pltpu.VMEM((8 * EDGE, d), bf16),
            pltpu.VMEM((mid_count + 8 * EDGE, d), bf16),
            pltpu.VMEM((8 * EDGE, d), bf16),
            pltpu.VMEM((coarse_padded + 8 * EDGE, d), bf16),
            pltpu.VMEM((8 * mid_count, d), bf16),
            pltpu.VMEM((8 * coarse_padded, d), bf16),
            dma((chunks,)), dma((4,)), dma((chunks,)), dma((chunks,)), dma((24,)), dma((24,)),
        ],
        compiler_params=pltpu.CompilerParams(
            vmem_limit_bytes=60 << 20, collective_id=0, has_side_effects=True
        ),
        name="sweep",
    )(
        fine_nodes.reshape(total, d), mid_nodes.reshape(mid_count, d), coarse_nodes, edge_flags,
        proc_weights, bridge_weights, proc_biases, *tables, *levels,
    )
    refined = pl.pallas_call(
        add_kernel,
        out_shape=jax.ShapeDtypeStruct((total, d), f32),
        in_specs=[anywhere, vmem, vmem],
        out_specs=anywhere,
        scratch_shapes=[pltpu.VMEM((total, d), f32), dma((chunks,)), dma((chunks,))],
        compiler_params=pltpu.CompilerParams(vmem_limit_bytes=60 << 20),
        name="add",
    )(one, spread, jnp.asarray(pool.T, bf16))
    return (refined.reshape(fine_nodes.shape), average.reshape(fine_nodes.shape))


def solution(mesh):
    placed = (
        P(None, "lat", "lon", None),
        P(None, "lat", "lon", None),
        P(None, "lat", "lon", None),
        P(None, "lat", "lon"),
        P(),
        P(),
        P(),
    )
    return jax.shard_map(
        local,
        mesh=mesh,
        in_specs=placed,
        out_specs=(P(None, "lat", "lon", None), P(None, "lat", "lon", None)),
        check_vma=False,
    )
```
